32 devices in a mesh: dp: 4 (over x, core), ctx: 4 (over z), fsdp: 2 (over y).
Axes of the slice: x: 2, y: 2, z: 4, core: 2. Of those that a mesh axis runs over, the one named last changes fastest.
Arguments:
- tokens: bfloat16 [16, 2048, 768], P(('dp', 'fsdp'), 'ctx'), may hold values from -6 to 6
- cotangent: bfloat16 [16, 2048, 768], P(('dp', 'fsdp'), 'ctx'), may hold values from -6 to 6
- qkv_weight: bfloat16 [768, 2304], P(('dp', 'fsdp')), may hold values from -8 to 8
- out_weight: bfloat16 [768, 768], P(('dp', 'fsdp')), may hold values from -0.75 to 0.75
- up_weight: bfloat16 [768, 2304], P(('dp', 'fsdp')), may hold values from -0.21875 to 0.21875
- down_weight: bfloat16 [1152, 768], P(('dp', 'fsdp')), may hold values from -0.1875 to 0.1875
- attention_gain: bfloat16 [768], P(('dp', 'fsdp')), may hold values from 0.25 to 1.75
- feedforward_gain: bfloat16 [768], P(('dp', 'fsdp')), may hold values from 0.25 to 1.75
Outputs:
- output: bfloat16 [16, 2048, 768], P(('dp', 'fsdp'), 'ctx')
- token_grad: float32 [16, 2048, 768], P(('dp', 'fsdp'), 'ctx')
- grad_qkv: float32 [768, 2304], P(('dp', 'fsdp'))
- grad_out: float32 [768, 768], P(('dp', 'fsdp'))
- grad_up: float32 [768, 2304], P(('dp', 'fsdp'))
- grad_down: float32 [1152, 768], P(('dp', 'fsdp'))
- grad_attention_gain: float32 [768], P(('dp', 'fsdp'))
- grad_feedforward_gain: float32 [768], P(('dp', 'fsdp'))
The draws below stay inside these ranges and needn't reach their ends.
All inputs are finite; a program needn't handle non-finite values.
Results may differ from the reference program's by a relative error of at most 0.02.
Values may be sent and summed in bfloat16 or wider, within the bound.
A program may use at most 320 MiB of HBM per device.

```python
import jax
import jax.numpy as jnp
from jax import lax

D = 768
HEADS = 12
HEAD = 64
FF = 1152
LEN = 2048
SEQS = 16


def draw_qkv_weight(key, part):
    value_key = jax.random.fold_in(jax.random.fold_in(key, 7), 0)
    spread = D ** (-0.5)
    entries = jnp.clip(jax.random.normal(value_key, (D, 3 * D), jnp.float32), -6.0, 6.0) * spread
    return entries.astype(jnp.bfloat16)


def level_of(stream_key, dims, cuts, least, top_value):
    level = 1.0
    for dim, shards_of in cuts:
        heights = jax.random.uniform(jax.random.fold_in(jax.random.fold_in(stream_key, 6), dim), (shards_of,), jnp.float32, least / len(cuts), top_value / len(cuts))
        level = level * jnp.repeat(jnp.exp(heights), dims[dim] // shards_of).reshape((-1,) + (1,) * (len(dims) - 1 - dim))
    return level


def normal_values(key, dims, width, most, shards=(), held_as=jnp.bfloat16):
    array = width * jax.random.normal(key, dims, jnp.float32)
    if shards:
        array = array * level_of(key, dims, shards, -0.22, 0.18)
    return jnp.clip(array, -most, most).astype(held_as)


def setup_inputs(seed: int = 0) -> dict:
    arg_keys = jax.random.split(jax.random.key(seed), 9)
    tokens = normal_values(arg_keys[0], (SEQS, LEN, D), 1.0, 6.0, ((0, 8), (1, 4)))
    cotangent = normal_values(arg_keys[1], (SEQS, LEN, D), 1.0, 6.0, ((0, 8), (1, 4)))
    qkv_weight = draw_qkv_weight(jax.random.fold_in(arg_keys[8], 71), 0)
    out_weight = normal_values(arg_keys[3], (D, D), HEAD ** -0.5, 0.75, ((0, 8),))
    up_weight = normal_values(arg_keys[4], (D, 2 * FF), D ** -0.5, 0.21875, ((0, 8),))
    down_weight = normal_values(arg_keys[5], (FF, D), FF ** -0.5, 0.1875, ((0, 8),))
    attention_gain = jnp.clip(1.0 + 0.15 * jax.random.normal(arg_keys[6], (D,), jnp.float32), 0.25, 1.75).astype(jnp.bfloat16)
    feedforward_gain = jnp.clip(1.0 + 0.15 * jax.random.normal(arg_keys[7], (D,), jnp.float32), 0.25, 1.75).astype(jnp.bfloat16)
    return {"tokens": tokens, "cotangent": cotangent, "qkv_weight": qkv_weight, "out_weight": out_weight, "up_weight": up_weight, "down_weight": down_weight, "attention_gain": attention_gain, "feedforward_gain": feedforward_gain}


norm_eps = 1e-05
rope_base = 160000.0

def layer_norm(values, norm_gain):
    centre = lax.optimization_barrier(jnp.mean(values, -1, keepdims=True))
    centred = values - centre
    inverse = lax.rsqrt(lax.optimization_barrier(jnp.mean(centred * centred, -1, keepdims=True)) + norm_eps)
    normed = centred * inverse
    return (normed, inverse, normed * norm_gain)

def norm_back(upstream, normed, inverse, norm_gain):
    scaled = upstream * norm_gain
    return (scaled - lax.optimization_barrier(jnp.mean(scaled, -1, keepdims=True)) - normed * lax.optimization_barrier(jnp.mean(scaled * normed, -1, keepdims=True))) * inverse

def gated_gelu(inputs, gating):
    return jax.nn.gelu(inputs, approximate=False) * gating

def rope_tables(positions, head_size):
    half_size = head_size // 2
    frequency = rope_base ** (-2.0 * jnp.arange(half_size, dtype=jnp.float32) / head_size)
    angles = positions.astype(jnp.float32)[:, None] * frequency[None, :]
    cosine = jnp.cos(angles)
    sine_half = jnp.sin(angles)
    return (jnp.concatenate([cosine, cosine], -1), jnp.concatenate([sine_half, sine_half], -1))

def rotate_heads(values, cosine_table, sine_table):
    half_size = values.shape[-1] // 2
    turned = jnp.concatenate([-values[..., half_size:], values[..., :half_size]], -1)
    return values * cosine_table[:, None, :] + turned * sine_table[:, None, :]

def rounded(values):
    return lax.optimization_barrier(values.astype(jnp.bfloat16)).astype(jnp.float32)

def attend_forward(query_rows, key_rows, value_rows):
    score_scale = HEAD ** (-0.5)
    scores = jnp.einsum('qhd,khd->hqk', query_rows.astype(jnp.float32), key_rows.astype(jnp.float32)) * score_scale
    highest = lax.optimization_barrier(jnp.max(scores, -1, keepdims=True))
    log_total = highest[..., 0] + jnp.log(lax.optimization_barrier(jnp.sum(jnp.exp(scores - highest), -1)))
    weights = rounded(jnp.exp(scores - log_total[..., None]))
    attended = jnp.einsum('hqk,khd->qhd', weights, value_rows.astype(jnp.float32))
    return (attended.astype(jnp.bfloat16), log_total)

def attend_backward(query_rows, key_rows, value_rows, attended, upstream, log_total):
    score_scale = HEAD ** (-0.5)
    query_wide = query_rows.astype(jnp.float32)
    key_wide = key_rows.astype(jnp.float32)
    value_wide = value_rows.astype(jnp.float32)
    upstream_wide = upstream.astype(jnp.float32)
    scores = jnp.einsum('qhd,khd->hqk', query_wide, key_wide) * score_scale
    weights = jnp.exp(scores - log_total[..., None])
    weight_grad = jnp.einsum('qhd,khd->hqk', upstream_wide, value_wide)
    delta_sum = jnp.transpose(lax.optimization_barrier(jnp.sum(upstream_wide * attended.astype(jnp.float32), -1)))
    score_grad = rounded(weights * (weight_grad - delta_sum[..., None]))
    query_grad = jnp.einsum('hqk,khd->qhd', score_grad, key_wide) * score_scale
    key_grad = jnp.einsum('hqk,qhd->khd', score_grad, query_wide) * score_scale
    value_grad = jnp.einsum('hqk,qhd->khd', rounded(weights), upstream_wide)
    return (query_grad, key_grad, value_grad)

def one_sequence(tokens, cotangent, qkv_weight, out_weight, up_weight, down_weight, attention_gain, feedforward_gain):
    length = tokens.shape[0]
    attn_gain = attention_gain.astype(jnp.float32)
    ffn_gain = feedforward_gain.astype(jnp.float32)
    inputs = tokens.astype(jnp.float32)
    normed_a, inverse_a, scaled_a = layer_norm(inputs, attn_gain)
    normal_a = scaled_a.astype(jnp.bfloat16)
    projected = jnp.dot(normal_a, qkv_weight, preferred_element_type=jnp.float32)
    cosine_table, sine_table = rope_tables(jnp.arange(length, dtype=jnp.int32), HEAD)
    head_shape = (length, HEADS, HEAD)
    query_rows = rotate_heads(projected[:, :D].reshape(head_shape), cosine_table, sine_table).astype(jnp.bfloat16)
    key_rows = rotate_heads(projected[:, D:2 * D].reshape(head_shape), cosine_table, sine_table).astype(jnp.bfloat16)
    value_rows = projected[:, 2 * D:].reshape(head_shape).astype(jnp.bfloat16)
    attended, log_total = attend_forward(query_rows, key_rows, value_rows)
    attended_flat = attended.reshape(length, D)
    residual = inputs + jnp.dot(attended_flat, out_weight, preferred_element_type=jnp.float32)
    normed_b, inverse_b, scaled_b = layer_norm(residual, ffn_gain)
    normal_b = scaled_b.astype(jnp.bfloat16)
    widened = jnp.dot(normal_b, up_weight, preferred_element_type=jnp.float32)
    hidden, hidden_back = jax.vjp(gated_gelu, widened[:, :FF], widened[:, FF:])
    hidden_low = hidden.astype(jnp.bfloat16)
    output = (residual + jnp.dot(hidden_low, down_weight, preferred_element_type=jnp.float32)).astype(jnp.bfloat16)
    down_grad = jnp.dot(hidden_low.T, cotangent, preferred_element_type=jnp.float32)
    hidden_grad = jnp.dot(cotangent, down_weight.T, preferred_element_type=jnp.float32)
    input_grad, gating_grad = hidden_back(hidden_grad)
    widened_grad = jnp.concatenate([input_grad, gating_grad], -1).astype(jnp.bfloat16)
    up_grad = jnp.dot(normal_b.T, widened_grad, preferred_element_type=jnp.float32)
    normal_b_grad = jnp.dot(widened_grad, up_weight.T, preferred_element_type=jnp.float32)
    ffn_gain_grad = lax.optimization_barrier(jnp.sum(normal_b_grad * normed_b, 0))
    residual_grad = cotangent.astype(jnp.float32) + norm_back(normal_b_grad, normed_b, inverse_b, ffn_gain)
    residual_low = residual_grad.astype(jnp.bfloat16)
    out_grad = jnp.dot(attended_flat.T, residual_low, preferred_element_type=jnp.float32)
    attended_grad = jnp.dot(residual_low, out_weight.T, preferred_element_type=jnp.float32).astype(jnp.bfloat16).reshape(head_shape)
    query_grad, key_grad, value_grad = attend_backward(query_rows, key_rows, value_rows, attended, attended_grad, log_total)
    query_grad = rotate_heads(query_grad, cosine_table, -sine_table)
    key_grad = rotate_heads(key_grad, cosine_table, -sine_table)
    projected_grad = jnp.concatenate([query_grad.reshape(length, D), key_grad.reshape(length, D), value_grad.reshape(length, D)], -1).astype(jnp.bfloat16)
    qkv_grad = jnp.dot(normal_a.T, projected_grad, preferred_element_type=jnp.float32)
    normal_a_grad = jnp.dot(projected_grad, qkv_weight.T, preferred_element_type=jnp.float32)
    attn_gain_grad = lax.optimization_barrier(jnp.sum(normal_a_grad * normed_a, 0))
    token_grad = residual_grad + norm_back(normal_a_grad, normed_a, inverse_a, attn_gain)
    return (output, token_grad, (qkv_grad, out_grad, up_grad, down_grad, attn_gain_grad, ffn_gain_grad))

def reference(tokens, cotangent, qkv_weight, out_weight, up_weight, down_weight, attention_gain, feedforward_gain):
    start_grads = (jnp.zeros(qkv_weight.shape, jnp.float32), jnp.zeros(out_weight.shape, jnp.float32), jnp.zeros(up_weight.shape, jnp.float32), jnp.zeros(down_weight.shape, jnp.float32), jnp.zeros((D,), jnp.float32), jnp.zeros((D,), jnp.float32))

    def advance(running, pair_now):
        output, token_grad, fresh = one_sequence(pair_now[0], pair_now[1], qkv_weight, out_weight, up_weight, down_weight, attention_gain, feedforward_gain)
        return (jax.tree.map(jnp.add, running, fresh), (output, token_grad))
    summed, (output, token_grad) = lax.scan(advance, start_grads, (tokens, cotangent))
    return (output, token_grad, summed[0], summed[1], summed[2], summed[3], summed[4], summed[5])
```

```python
from functools import partial
import math

import jax
import jax.numpy as jnp
from jax import lax
from jax.experimental import pallas as pl
from jax.experimental.pallas import tpu as pltpu
from jax.sharding import PartitionSpec as P

D = 768
HEADS = 12
HEAD = 64
FF = 1152
HALF = HEAD // 2

norm_eps = 1e-05
rope_base = 160000.0
score_scale = HEAD ** (-0.5)
score_base2 = score_scale * math.log2(math.e)
WEIGHT_AXES = ("dp", "fsdp")
f32 = jnp.float32
bf16 = jnp.bfloat16


def dot(left, right, left_dim=1, right_dim=0):
    return lax.dot_general(
        left, right, (((left_dim,), (right_dim,)), ((), ())), preferred_element_type=f32
    )


def layer_norm(values, norm_gain):
    centre = jnp.mean(values, -1, keepdims=True)
    centred = values - centre
    inverse = lax.rsqrt(jnp.mean(centred * centred, -1, keepdims=True) + norm_eps)
    normed = centred * inverse
    return (normed, inverse, normed * norm_gain)


def norm_back(upstream, normed, inverse, norm_gain):
    scaled = upstream * norm_gain
    return (
        scaled
        - jnp.mean(scaled, -1, keepdims=True)
        - normed * jnp.mean(scaled * normed, -1, keepdims=True)
    ) * inverse


def gated_gelu(inputs, gating):
    return jax.nn.gelu(inputs, approximate=False) * gating


def rope_rows(length):
    frequency = rope_base ** (-2.0 * jnp.arange(HALF, dtype=f32) / HEAD)
    angles = frequency[:, None] * jnp.arange(length, dtype=jnp.int32).astype(f32)[None, :]
    return (jnp.cos(angles), jnp.sin(angles))


def chunk_of(length, most):
    return most if length % most == 0 else length


def forward_kernel(q_ref, k_ref, v_ref, o_ref, log_ref, k_rows, v_wide):
    length = k_ref.shape[-1]
    chunk = chunk_of(length, 512)

    @pl.when(pl.program_id(1) == 0)
    def _():
        k_rows[...] = k_ref[0, 0].T
        v_wide[:HEAD, :] = v_ref[0, 0]
        v_wide[HEAD:, :] = jnp.ones((v_wide.shape[0] - HEAD, length), bf16)

    query = q_ref[0, 0]
    highest = None
    total = None
    for start in range(0, length, chunk):
        scores = dot(k_rows[start : start + chunk, :], query) * score_base2
        top = jnp.max(scores, 0, keepdims=True)
        new_high = top if highest is None else jnp.maximum(highest, top)
        weights = jnp.exp2(scores - new_high).astype(bf16)
        term = dot(v_wide[:, start : start + chunk], weights)
        total = term if total is None else total * jnp.exp2(highest - new_high) + term
        highest = new_high
    denominator = total[HEAD : HEAD + 1, :]
    o_ref[0, 0] = (total[:HEAD, :] / denominator).astype(bf16)
    log_ref[0] = highest + jnp.log2(denominator)


def attend(heads_t, block_len):
    _, count, _, length = heads_t.shape
    blocks = length // block_len
    return pl.pallas_call(
        forward_kernel,
        grid=(count, blocks),
        in_specs=[
            pl.BlockSpec((1, 1, HEAD, block_len), lambda h, c: (0, h, 0, c)),
            pl.BlockSpec((1, 1, HEAD, length), lambda h, c: (1, h, 0, 0)),
            pl.BlockSpec((1, 1, HEAD, length), lambda h, c: (2, h, 0, 0)),
        ],
        out_specs=[
            pl.BlockSpec((1, 1, HEAD, block_len), lambda h, c: (c, h, 0, 0)),
            pl.BlockSpec((1, 1, block_len), lambda h, c: (h, 0, c)),
        ],
        out_shape=[
            jax.ShapeDtypeStruct((blocks, count, HEAD, block_len), bf16),
            jax.ShapeDtypeStruct((count, 1, length), f32),
        ],
        scratch_shapes=[
            pltpu.VMEM((length, HEAD), bf16),
            pltpu.VMEM((HEAD + 16, length), bf16),
        ],
        compiler_params=pltpu.CompilerParams(vmem_limit_bytes=40 << 20),
        cost_estimate=pl.CostEstimate(
            flops=16 * count * length * length * HEAD,
            bytes_accessed=10 * count * length * HEAD,
            transcendentals=count * length * length,
        ),
    )(heads_t, heads_t, heads_t)


def rope_back(grad_t, cosine, sine):
    first, second = grad_t[:HALF, :], grad_t[HALF:, :]
    return (first * cosine + second * sine, second * cosine - first * sine)


def backward_kernel(
    q_ref, k_ref, v_ref, o_ref, up_ref, log_ref, cos_all, sin_all, cos_ref, sin_ref,
    dq_ref, dk_ref, dv_ref, q_rows, up_rows, up_cols, delta, dq_sum,
):
    step = pl.program_id(1)
    blocks, block_len = up_ref.shape[0], up_ref.shape[-1]
    length = q_ref.shape[-1]
    chunk = chunk_of(length, 512)

    @pl.when(step == 0)
    def _():
        q_rows[...] = q_ref[0, 0].T
        for number in range(blocks):
            place = slice(number * block_len, (number + 1) * block_len)
            upstream = up_ref[number, 0]
            up_cols[:, place] = upstream
            up_rows[place, :] = upstream.T
            delta[:, place] = jnp.sum(
                upstream.astype(f32) * o_ref[number, 0].astype(f32), 0, keepdims=True
            )
        dq_sum[...] = jnp.zeros_like(dq_sum)

    key_t = k_ref[0, 0]
    key = key_t.T
    value = v_ref[0, 0].T
    dk = None
    dv = None
    for start in range(0, length, chunk):
        place = slice(start, start + chunk)
        scores = dot(key, q_ref[0, 0, :, place]) * score_base2
        weights = jnp.exp2(scores - log_ref[0, :, place])
        weight_grad = dot(value, up_cols[:, place])
        score_grad = (weights * (weight_grad - delta[:, place])).astype(bf16)
        dv_term = dot(weights.astype(bf16), up_rows[place, :])
        dk_term = dot(score_grad, q_rows[place, :])
        dv = dv_term if dv is None else dv + dv_term
        dk = dk_term if dk is None else dk + dk_term
        dq_sum[:, place] += dot(key_t, score_grad)
    upper, lower = rope_back((dk * score_scale).T, cos_ref[...], sin_ref[...])
    dk_ref[0, :HALF, :] = upper.astype(bf16)
    dk_ref[0, HALF:, :] = lower.astype(bf16)
    dv_ref[0] = dv.T.astype(bf16)

    @pl.when(step == pl.num_programs(1) - 1)
    def _():
        upper, lower = rope_back(dq_sum[...] * score_scale, cos_all[...], sin_all[...])
        dq_ref[0, :HALF, :] = upper.astype(bf16)
        dq_ref[0, HALF:, :] = lower.astype(bf16)


def attend_back(heads_t, attended, upstream, log_total, cosine, sine):
    _, count, _, length = heads_t.shape
    blocks, _, _, block_len = attended.shape
    rows = chunk_of(length, 256)
    split = pl.BlockSpec((blocks, 1, HEAD, block_len), lambda h, k: (0, h, 0, 0))
    shape = jax.ShapeDtypeStruct((count, HEAD, length), bf16)
    return pl.pallas_call(
        backward_kernel,
        grid=(count, length // rows),
        in_specs=[
            pl.BlockSpec((1, 1, HEAD, length), lambda h, k: (0, h, 0, 0)),
            pl.BlockSpec((1, 1, HEAD, rows), lambda h, k: (1, h, 0, k)),
            pl.BlockSpec((1, 1, HEAD, rows), lambda h, k: (2, h, 0, k)),
            split,
            split,
            pl.BlockSpec((1, 1, length), lambda h, k: (h, 0, 0)),
            pl.BlockSpec((HALF, length), lambda h, k: (0, 0)),
            pl.BlockSpec((HALF, length), lambda h, k: (0, 0)),
            pl.BlockSpec((HALF, rows), lambda h, k: (0, k)),
            pl.BlockSpec((HALF, rows), lambda h, k: (0, k)),
        ],
        out_specs=[
            pl.BlockSpec((1, HEAD, length), lambda h, k: (h, 0, 0)),
            pl.BlockSpec((1, HEAD, rows), lambda h, k: (h, 0, k)),
            pl.BlockSpec((1, HEAD, rows), lambda h, k: (h, 0, k)),
        ],
        out_shape=[shape, shape, shape],
        scratch_shapes=[
            pltpu.VMEM((length, HEAD), bf16),
            pltpu.VMEM((length, HEAD), bf16),
            pltpu.VMEM((HEAD, length), bf16),
            pltpu.VMEM((1, length), f32),
            pltpu.VMEM((HEAD, length), f32),
        ],
        compiler_params=pltpu.CompilerParams(vmem_limit_bytes=40 << 20),
        cost_estimate=pl.CostEstimate(
            flops=40 * count * length * length * HEAD,
            bytes_accessed=16 * count * length * HEAD,
            transcendentals=count * length * length,
        ),
    )(heads_t, heads_t, heads_t, attended, upstream, log_total, cosine, sine, cosine, sine)


def gather_rows(shard):
    return lax.all_gather(shard, WEIGHT_AXES, axis=0, tiled=True)


def exchange(blocks):
    return lax.all_to_all(blocks, "ctx", 0, 0, tiled=True)


def body(
    tokens,
    cotangent,
    qkv_weight,
    out_weight,
    up_weight,
    down_weight,
    attention_gain,
    feedforward_gain,
):
    ctx = lax.axis_size("ctx")
    groups = lax.axis_size("dp") * lax.axis_size("fsdp")
    seq_count, block_len = (tokens.shape[0], tokens.shape[1])
    length = block_len * ctx
    own = -(-HEADS // ctx)
    width = own * HEAD
    spare = ctx * own - HEADS
    shard_rows = qkv_weight.shape[0]
    by_head = qkv_weight.reshape(shard_rows, 3, D)
    if spare:
        by_head = jnp.pad(by_head, ((0, 0), (0, 0), (0, spare * HEAD)))
    own_columns = lax.dynamic_slice_in_dim(by_head, lax.axis_index("ctx") * width, width, 2)
    gains = gather_rows(jnp.stack([attention_gain, feedforward_gain], -1)).astype(f32)
    attn_gain, ffn_gain = (gains[:, 0], gains[:, 1])
    qkv_own = gather_rows(own_columns.reshape(shard_rows, 3 * width))
    gathered = [
        lax.all_gather(tokens[number], "ctx", axis=0, tiled=True) for number in range(seq_count)
    ]
    out_whole = gather_rows(out_weight)
    up_whole = gather_rows(up_weight)
    down_whole = gather_rows(down_weight)
    cosine, sine = rope_rows(length)

    saved = []
    for number in range(seq_count):
        normal = layer_norm(gathered[number].astype(f32), attn_gain)[2].astype(bf16)
        projected = dot(qkv_own, normal, 0, 1).reshape(3, own, 2, HALF, length)
        first, second = (projected[:2, :, 0], projected[:2, :, 1])
        turned = jnp.stack([first * cosine - second * sine, second * cosine + first * sine], 2)
        heads_t = (
            jnp.concatenate([turned, projected[2:]], 0).astype(bf16).reshape(3, own, HEAD, length)
        )
        attended, log_total = attend(heads_t, block_len)
        saved.append((normal, heads_t, attended, log_total, exchange(attended)))

    outputs = []
    middle = []
    up_grad = down_grad = out_grad = 0.0
    for number in range(seq_count):
        attended_t = saved[number][4].reshape(ctx * width, block_len)[:D]
        inputs = tokens[number].astype(f32)
        residual = inputs + dot(attended_t, out_whole, 0, 0)
        normed_b, inverse_b, scaled_b = layer_norm(residual, ffn_gain)
        normal_b = scaled_b.astype(bf16)
        widened = dot(normal_b, up_whole)
        hidden, hidden_back = jax.vjp(gated_gelu, widened[:, :FF], widened[:, FF:])
        hidden_low = hidden.astype(bf16)
        outputs.append((residual + dot(hidden_low, down_whole)).astype(bf16))
        upstream = cotangent[number]
        hidden_grad = dot(upstream, down_whole, 1, 1)
        input_grad, gating_grad = hidden_back(hidden_grad)
        widened_grad = jnp.concatenate([input_grad, gating_grad], -1).astype(bf16)
        normal_b_grad = dot(widened_grad, up_whole, 1, 1)
        residual_grad = upstream.astype(f32) + norm_back(
            normal_b_grad, normed_b, inverse_b, ffn_gain
        )
        residual_low = residual_grad.astype(bf16)
        attended_grad = dot(out_whole, residual_low, 1, 1).astype(bf16)
        if spare:
            attended_grad = jnp.pad(attended_grad, ((0, spare * HEAD), (0, 0)))
        middle.append(
            (residual_grad, exchange(attended_grad.reshape(ctx, own, HEAD, block_len)))
        )
        down_grad = down_grad + dot(hidden_low, upstream, 0, 0)
        up_grad = up_grad + dot(normal_b, widened_grad, 0, 0)
        out_grad = out_grad + dot(attended_t, residual_low)

    parts = [up_grad[:, start : start + D] for start in range(0, up_grad.shape[1], D)]
    parts += [down_grad, out_grad]
    packed = jnp.concatenate([part.astype(bf16).reshape(groups, -1, D) for part in parts], 1)
    shard = lax.psum_scatter(packed, WEIGHT_AXES, scatter_dimension=0, tiled=True)[0]
    shard = lax.psum(shard, "ctx").astype(f32)
    cuts = []
    offset = 0
    for part in parts:
        rows = part.shape[0] // groups
        cuts.append(shard[offset : offset + rows])
        offset += rows
    up_shard = jnp.concatenate(cuts[:-2], -1)
    down_shard, out_shard = cuts[-2:]

    token_grads = []
    qkv_grad = 0.0
    for number in range(seq_count):
        normal, heads_t, attended, log_total, _ = saved[number]
        residual_grad, upstream_t = middle[number]
        pieces = attend_back(heads_t, attended, upstream_t, log_total, cosine, sine)
        projected_grad = jnp.concatenate(pieces, 0).reshape(3 * width, length)
        partial_grad = dot(projected_grad, qkv_own, 0, 1).astype(bf16)
        normal_a_grad = lax.psum_scatter(
            partial_grad, "ctx", scatter_dimension=0, tiled=True
        ).astype(f32)
        qkv_grad = qkv_grad + dot(normal, projected_grad, 0, 1)
        normed_a, inverse_a, _ = layer_norm(tokens[number].astype(f32), attn_gain)
        token_grads.append(
            residual_grad + norm_back(normal_a_grad, normed_a, inverse_a, attn_gain)
        )
    qkv_cut = lax.psum_scatter(
        qkv_grad.astype(bf16), WEIGHT_AXES, scatter_dimension=0, tiled=True
    )
    qkv_all = lax.all_gather(qkv_cut, "ctx", axis=0).astype(f32)
    qkv_shard = jnp.transpose(qkv_all.reshape(ctx, shard_rows, 3, width), (1, 2, 0, 3)).reshape(
        shard_rows, 3, ctx * width
    )[:, :, :D].reshape(shard_rows, 3 * D)
    attn_gain_grad = jnp.sum(qkv_weight.astype(f32) * qkv_shard, -1) / attention_gain.astype(f32)
    ffn_gain_grad = jnp.sum(up_weight.astype(f32) * up_shard, -1) / feedforward_gain.astype(f32)
    return (
        jnp.stack(outputs),
        jnp.stack(token_grads),
        qkv_shard,
        out_shard,
        up_shard,
        down_shard,
        attn_gain_grad,
        ffn_gain_grad,
    )


def solution(mesh):
    rows = P(("dp", "fsdp"), "ctx", None)
    weight = P(("dp", "fsdp"), None)
    gain = P(("dp", "fsdp"))
    return jax.shard_map(
        body,
        mesh=mesh,
        in_specs=(rows, rows, weight, weight, weight, weight, gain, gain),
        out_specs=(rows, rows, weight, weight, weight, weight, gain, gain),
        check_vma=False,
    )
```
